256 devices in a mesh: sec: 16 (over z, core), patch: 16 (over x, y).
Axes of the slice: x: 4, y: 4, z: 8, core: 2. Of those that a mesh axis runs over, the one named last changes fastest.
Arguments:
- rhs: bfloat16 [24, 1572864], P(None, ('sec', 'patch')), may hold values from -6 to 6
- curl_blocks: bfloat16 [16384, 4, 9216], P(('sec', 'patch')), may hold values from -0.3125 to 0.3125
- block_cols: int32 [16384, 4], P(('sec', 'patch')), may hold values from 0 to 63
- hole_mask: int32 [16384], P(('sec', 'patch')), may hold values 0 or 1
- edge_flip: int32 [1572864], P(('sec', 'patch')), may hold values from 0 to 1
- send_list: int32 [16, 16, 16, 8], P('sec', 'patch'), may hold values from 0 to 63
- send_count: int32 [16, 16, 16], P('sec', 'patch'), may hold values from 5 to 8
- recv_list: int32 [16, 16, 16, 8], P('sec', 'patch'), may hold values from 0 to 63
- dtn_blocks: bfloat16 [16, 16, 16, 8, 9216], P('sec', 'patch'), may hold values from -0.4375 to 0.4375
Outputs:
- state: float32 [24, 1572864], P(None, ('sec', 'patch'))
The draws below stay inside these ranges and needn't reach their ends.
Inputs may be any that keep to these rules, and one draw needn't show every extreme that they name: Slots f >= send_count carry no block.
All inputs are finite; a program needn't handle non-finite values. No bound on the sum of `hole_mask` on one device may be relied on, other than what follows from the above.
Results may differ from the reference program's by a relative error of at most 0.029.
Values may be sent and summed in bfloat16 or wider, within the bound.
A program may use at most 64 MiB of HBM per device.

```python
import jax
import jax.numpy as jnp
from jax import lax

BS = 96
COLS = 24
NB = 64
K = 4
F = 8
NI = 8
ITERS = 8
TICKS = 2
BLOCKS = 16384
EDGES = 1572864
N_SEC = 16
N_PATCH = 16


def with_ends(entries, stream_key, least, top_value):
    place = [jax.random.randint(jax.random.fold_in(stream_key, axis), (), 0, length) for axis, length in enumerate(entries.shape)]
    widest = entries.shape.index(max(entries.shape))
    next_to = place[:widest] + [(place[widest] + 1) % entries.shape[widest]] + place[widest + 1:]
    return entries.at[tuple(place)].set(least).at[tuple(next_to)].set(top_value)


def block_scale(rng, extent, shards, smallest, top_value):
    level, own = 1.0, jax.random.fold_in(rng, 6)
    for dim, shards_of in shards:
        draws = jnp.exp(jax.random.uniform(jax.random.fold_in(own, dim), (shards_of,), jnp.float32, smallest / len(shards), top_value / len(shards)))
        level = level * jnp.repeat(draws, extent[dim] // shards_of).reshape([-1 if axis == dim else 1 for axis in range(len(extent))])
    return level


def normal_values(rng, extent, scale, bound, shards=(), kind=jnp.bfloat16):
    level = block_scale(rng, extent, shards, -0.22, 0.18) if shards else 1.0
    drawn = jax.random.normal(rng, extent, jnp.float32) * scale * level
    return jnp.minimum(jnp.maximum(drawn, -bound), bound).astype(kind)


def setup_inputs(seed: int = 0) -> dict:
    streams_of = jax.random.split(jax.random.key(seed), 10)
    return {
        "rhs": normal_values(streams_of[0], (COLS, EDGES), 1.0, 6.0, ((1, 256),)),
        "curl_blocks": normal_values(streams_of[1], (BLOCKS, K, BS * BS), (K * BS) ** -0.5, 0.3125, ((0, 256),)),
        "block_cols": with_ends(jax.random.randint(streams_of[2], (BLOCKS, K), 0, NB), jax.random.fold_in(streams_of[2], 1), 0, NB - 1).astype(jnp.int32),
        "hole_mask": with_ends((jax.random.randint(streams_of[3], (BLOCKS,), 0, 8) < 7).astype(jnp.int32), jax.random.fold_in(streams_of[3], 1), 0, 1),
        "edge_flip": with_ends(jax.random.randint(streams_of[4], (EDGES,), 0, 2), jax.random.fold_in(streams_of[4], 1), 0, 1).astype(jnp.int32),
        "send_list": with_ends(jax.random.randint(streams_of[5], (N_SEC, N_PATCH, N_PATCH, F), 0, NB), jax.random.fold_in(streams_of[5], 1), 0, NB - 1).astype(jnp.int32),
        "send_count": with_ends(jax.random.randint(streams_of[6], (N_SEC, N_PATCH, N_PATCH), F - F // 4 - 1, F + 1), jax.random.fold_in(streams_of[6], 1), F - F // 4 - 1, F).astype(jnp.int32),
        "recv_list": with_ends(jax.random.randint(streams_of[7], (N_SEC, N_PATCH, N_PATCH, F), 0, NB), jax.random.fold_in(streams_of[7], 1), 0, NB - 1).astype(jnp.int32),
        "dtn_blocks": normal_values(streams_of[8], (N_SEC, N_PATCH, N_PATCH, F, BS * BS), (2 * BS) ** -0.5, 0.4375, ((0, 16), (1, 16))),
    }


def apply_curl(matrices, columns, state_bf):
    nearby = state_bf[:, columns]
    return jnp.einsum('nked,cnkd->cne', matrices.astype(jnp.float32), nearby, precision=lax.Precision.HIGHEST)


def apply_faces(received, dtn_mats, onehot):
    products = jnp.einsum('qfed,qfcd->qfce', dtn_mats.astype(jnp.float32), received, precision=lax.Precision.HIGHEST)
    products = lax.optimization_barrier(products.astype(jnp.bfloat16)).astype(jnp.float32)
    return jnp.einsum('qfn,qfce->cne', onehot, products, precision=lax.Precision.HIGHEST)


def pick_rows(table, index):
    return table[index]


def reference(rhs, curl_blocks, block_cols, hole_mask, edge_flip, send_list, send_count, recv_list, dtn_blocks):
    coupling = 0.85
    devs = N_SEC * N_PATCH
    source = rhs.astype(jnp.float32).reshape(COLS, N_SEC, N_PATCH, NB, BS).transpose(1, 2, 0, 3, 4)
    matrices = curl_blocks.reshape(devs, NB, K, BS, BS)
    columns = block_cols.reshape(devs, NB, K)
    keepers = hole_mask.reshape(N_SEC, N_PATCH, 1, NB, 1).astype(jnp.float32)
    edge_sign = (1 - 2 * edge_flip).astype(jnp.float32).reshape(N_SEC, N_PATCH, NB, BS)
    dtn_mats = dtn_blocks.reshape(devs, N_PATCH, F, BS, BS)
    filled = (jnp.arange(F)[None, None, None, :] < send_count[..., None]).astype(jnp.float32)
    onehot = (recv_list[..., None] == jnp.arange(NB)[None, None, None, None, :]).astype(jnp.float32)
    onehot = onehot.reshape(devs, N_PATCH, F, NB)
    state = keepers * source
    from_left = jnp.zeros((N_SEC, N_PATCH, COLS, NI, BS), jnp.float32)
    from_right = jnp.zeros((N_SEC, N_PATCH, COLS, NI, BS), jnp.float32)
    for segment in range(TICKS):
        state_bf = lax.optimization_barrier(state.astype(jnp.bfloat16)).astype(jnp.float32)
        by_block = state_bf.transpose(0, 1, 3, 2, 4)
        picked = jax.vmap(jax.vmap(pick_rows))(by_block, send_list)
        flips = jax.vmap(jax.vmap(pick_rows))(edge_sign, send_list)
        sent = picked * flips[:, :, :, :, None, :] * filled[..., None, None]
        received = sent.transpose(0, 2, 1, 3, 4, 5).reshape(devs, N_PATCH, F, COLS, BS)
        face_terms = lax.map(lambda group: apply_faces(group[0], group[1], group[2]), (received, dtn_mats, onehot))
        forcing = source + face_terms.reshape(N_SEC, N_PATCH, COLS, NB, BS)
        forcing = forcing.at[:, :, :, :NI].add(from_left)
        forcing = forcing.at[:, :, :, NB - NI:].add(from_right)
        for sweep_idx in range(ITERS):
            state_bf = lax.optimization_barrier(state.astype(jnp.bfloat16)).astype(jnp.float32)
            image = lax.map(lambda group: apply_curl(group[0], group[1], group[2]), (matrices, columns, state_bf.reshape(devs, COLS, NB, BS)))
            state = keepers * (forcing - coupling * image.reshape(N_SEC, N_PATCH, COLS, NB, BS))
        if segment < TICKS - 1:
            to_right = lax.optimization_barrier(state[:, :, :, NB - NI:].astype(jnp.bfloat16)).astype(jnp.float32)
            to_left = lax.optimization_barrier(state[:, :, :, :NI].astype(jnp.bfloat16)).astype(jnp.float32)
            from_left = jnp.concatenate([jnp.zeros_like(to_right[:1]), to_right[:-1]], axis=0)
            from_right = jnp.concatenate([to_left[1:], jnp.zeros_like(to_left[:1])], axis=0)
    return state.transpose(2, 0, 1, 3, 4).reshape(COLS, EDGES)
```

```python
import jax
import jax.numpy as jnp
from jax import lax
from jax.experimental import pallas as pl
from jax.experimental.pallas import tpu as pltpu
from jax.sharding import PartitionSpec as P

BS = 96
COLS = 24
NB = 64
K = 4
F = 8
NI = 8
ITERS = 8
TICKS = 2
LANES = 128
ROWS = BS * BS // LANES
GROUP = 4
GROUPS = NB // GROUP
PACK = 2 * 3 * COLS
COUPLING = 0.85
CHUNKS = 16
UNROLL = 64

f32 = jnp.float32
bf16 = jnp.bfloat16
NN = (((1,), (0,)), ((), ()))


def lanes_of(shape):
    return lax.broadcasted_iota(jnp.int32, shape, len(shape) - 1)


def split4(a, b, c):
    lane = lanes_of(a.shape)
    return (
        a,
        pltpu.roll(jnp.where(lane >= 96, a, b), 32, 1),
        pltpu.roll(jnp.where(lane >= 64, b, c), 64, 1),
        pltpu.roll(c, 96, 1),
    )


def join4(w, x, y, z):
    lane = lanes_of(w.shape)
    x = pltpu.roll(x, 96, 1)
    y = pltpu.roll(y, 64, 1)
    z = pltpu.roll(z, 32, 1)
    return jnp.where(lane < 96, w, x), jnp.where(lane < 64, x, y), jnp.where(lane < 32, y, z)


def kernel(
    peers, sections,
    rhs, flip, cols, hole, slist, scount, rlist, curl, dtn, out,
    abuf, dbuf, wide, square, mats, dmats, src, frc, img, st0, st1, signed, sign, signrow,
    prod, face, onehot, sendbuf, recvbuf, isend, irecv,
    csem, dsem, ssem, rsem, issem, irsem,
):
    me = lax.axis_index("patch")
    sec = lax.axis_index("sec")

    curl_copies = lambda i: pltpu.make_async_copy(
        curl.at[pl.ds(i * (NB // CHUNKS), NB // CHUNKS)],
        abuf.at[pl.ds(i * (NB // CHUNKS), NB // CHUNKS)],
        csem.at[i],
    )
    dtn_copies = lambda i: pltpu.make_async_copy(dtn.at[i], dbuf.at[i], dsem.at[i])

    irecv[...] = jnp.zeros_like(irecv)
    barrier = pltpu.get_barrier_semaphore()
    for d in range(1, peers):
        pl.semaphore_signal(
            barrier, inc=1, device_id={"patch": lax.rem(me + d, peers)}, device_id_type=pl.DeviceIdType.MESH
        )

    for d in (1, sections - 1):
        pl.semaphore_signal(
            barrier, inc=1, device_id={"sec": lax.rem(sec + d, sections)}, device_id_type=pl.DeviceIdType.MESH
        )

    for i in range(CHUNKS):
        curl_copies(i).start()
    for i in range(peers):
        dtn_copies(i).start()

    signrow[...] = (1 - 2 * flip[...]).astype(f32)
    parts = [signrow[pl.ds(t, GROUPS, stride=3), :] for t in range(3)]
    for r, row in enumerate(split4(*parts)):
        sign[pl.ds(r, GROUPS, stride=4), :] = row

    for i in range(GROUPS):
        parts = [rhs[:, pl.ds(384 * i + LANES * t, LANES)].astype(f32) for t in range(3)]
        for r, row in enumerate(split4(*parts)):
            n = GROUP * i + r
            kept = row * hole[n].astype(f32)
            src[n] = row
            st0[n] = kept.astype(bf16)
            signed[n] = kept * sign[n : n + 1, :]

    pl.semaphore_wait(barrier, peers + 1)

    def face_copy(tick, d):
        return pltpu.make_async_remote_copy(
            src_ref=sendbuf.at[tick, d],
            dst_ref=recvbuf.at[tick, d],
            send_sem=ssem.at[tick, d],
            recv_sem=rsem.at[tick, d],
            device_id={"patch": lax.rem(me + d, peers)},
            device_id_type=pl.DeviceIdType.MESH,
        )

    def packed(q):
        pieces = []
        for half in range(2):
            blocks = []
            for j in range(GROUP):
                f = GROUP * half + j
                used = jnp.where(f < scount[0, q], 1.0, 0.0).astype(f32)
                blocks.append(signed[slist[f, q]] * used)
            pieces.extend(join4(*blocks))
        return jnp.concatenate(pieces, axis=0).astype(bf16)

    def send_faces(tick):
        def one(d, carry):
            sendbuf[tick, d] = packed(lax.rem(me + d, peers))
            face_copy(tick, d).start()
            return carry

        lax.fori_loop(1, peers, one, 0)
        recvbuf[tick, 0] = packed(me)

    def gather(state, n):
        lane = lanes_of((COLS, LANES))
        last = state[cols[3, n]]
        return jnp.concatenate(
            [jnp.where(lane < BS, state[cols[k, n]], pltpu.roll(last, 96 - 32 * k, 1)) for k in range(3)], axis=1
        )

    def image(state, n):
        return lax.dot_general(gather(state, n), mats[n], NN, preferred_element_type=f32)

    def over_blocks(body):
        if UNROLL == NB:
            for store in [body(n) for n in range(NB)]:
                store()
            return

        def batch(i, carry):
            for store in [body(i * UNROLL + u) for u in range(UNROLL)]:
                store()
            return carry

        lax.fori_loop(0, NB // UNROLL, batch, 0)

    def first_image(state):
        def body(n):
            value = image(state, n)

            def store():
                img[n] = value

            return store

        over_blocks(body)

    def sweep(before, after, dtype):
        def body(n):
            value = frc[n] - (COUPLING * hole[n].astype(f32)) * image(before, n)

            def store():
                after[n] = value.astype(dtype)

            return store

        over_blocks(body)

    def relayout_matrices():
        def transposed(base, count, stride, slot):
            parts = [wide[slot, pl.ds(base + stride * t, COLS, stride=3 * stride), :] for t in range(3)]
            for r, row in enumerate(split4(*parts)):
                square[count, pl.ds(r, COLS, stride=4), :] = row
            return lambda: square[count].T[:BS].astype(bf16)

        per = NB // CHUNKS

        def curl_chunk(i, carry):
            curl_copies(i).wait()
            for u in range(per):
                wide[u] = abuf[i * per + u].astype(f32)
            later = [[transposed(k, u * K + k, K, u) for k in range(K)] for u in range(per)]
            for u in range(per):
                n = i * per + u
                for k in range(3):
                    mats[n, LANES * k : LANES * k + BS, :BS] = later[u][k]()
                tail = later[u][3]()
                for k in range(3):
                    mats[n, LANES * k + BS : LANES * (k + 1), :BS] = tail[32 * k : 32 * k + 32]
            return carry

        lax.fori_loop(0, CHUNKS, curl_chunk, 0)

        def dtn_chunk(i, carry):
            for u in range(2):
                dtn_copies(2 * i + u).wait()
            for u in range(2):
                for v in range(2):
                    wide[2 * u + v] = dbuf[2 * i + u, pl.ds(288 * v, 288)].astype(f32)
            later = []
            for u in range(2):
                for f in range(F):
                    parts = []
                    for t in range(3):
                        halves = [
                            wide[2 * u + v, pl.ds(f + F * t, COLS // 2, stride=3 * F), :] for v in range(2)
                        ]
                        parts.append(halves)
                    count = u * F + f
                    for v in range(2):
                        for r, row in enumerate(split4(*[p[v] for p in parts])):
                            square[count, pl.ds(48 * v + r, COLS // 2, stride=4), :] = row
                    later.append(count)
            for u in range(2):
                for f in range(F):
                    dmats[2 * i + u, f, :, :BS] = square[u * F + f].T[:BS].astype(bf16)
            return carry

        lax.fori_loop(0, peers // 2, dtn_chunk, 0)

        lane = lanes_of((1, LANES))
        target = jnp.zeros((1, LANES), jnp.int32)
        for q in range(peers):
            for f in range(F):
                target = jnp.where(lane == q * F + f, rlist[f, q], target)
        rows = lax.broadcasted_iota(jnp.int32, (NB, LANES), 0)
        onehot[...] = jnp.where(rows == target, 1.0, 0.0).astype(bf16)

    def face_products(tick):
        def one(d, carry):
            @pl.when(d > 0)
            def _():
                face_copy(tick, d).wait_recv()

            q = lax.rem(me + peers - d, peers)
            got = recvbuf[tick, d].astype(f32)
            for half in range(2):
                base = 72 * half
                rows = split4(got[base : base + 24], got[base + 24 : base + 48], got[base + 48 : base + 72])
                for j in range(GROUP):
                    f = GROUP * half + j
                    value = lax.dot_general(
                        rows[j].astype(bf16)[:, :BS], dmats[q, f], NN, preferred_element_type=f32
                    )
                    prod[pl.ds(q * F + f, COLS, stride=LANES), :] = value.astype(bf16).astype(f32)
            return carry

        lax.fori_loop(0, peers, one, 0)

        def column(c, carry):
            for u in range(4):
                base = pl.multiple_of((4 * c + u) * LANES, LANES)
                to = pl.multiple_of((4 * c + u) * NB, NB)
                face[pl.ds(to, NB), :] = lax.dot_general(
                    onehot[...], prod[pl.ds(base, LANES), :].astype(bf16), NN, preferred_element_type=f32
                )
            return carry

        lax.fori_loop(0, COLS // 4, column, 0)

    def first_update(tick, after):
        def block(n, extra):
            kept = hole[n].astype(f32)
            forcing = src[n] + face[pl.ds(n, COLS, stride=NB), :]
            if extra is not None:
                forcing = forcing + extra
            forcing = kept * forcing
            frc[n] = forcing
            after[n] = (forcing - (COUPLING * kept) * img[n]).astype(bf16)

        if tick == 0:
            for n in range(NB):
                block(n, None)
        else:
            for side, first in ((0, 0), (1, NB - NI)):
                got = irecv[side].astype(f32)
                for half in range(2):
                    base = 72 * half
                    rows = split4(got[base : base + 24], got[base + 24 : base + 48], got[base + 48 : base + 72])
                    for j in range(GROUP):
                        block(first + GROUP * half + j, rows[j])
            for n in range(NI, NB - NI):
                block(n, None)

    def interface_copy(side):
        return pltpu.make_async_remote_copy(
            src_ref=isend.at[side],
            dst_ref=irecv.at[side],
            send_sem=issem.at[side],
            recv_sem=irsem.at[side],
            device_id={"sec": sec + 1 if side == 0 else sec - 1},
            device_id_type=pl.DeviceIdType.MESH,
        )

    def send_interfaces(state):
        for side, first in ((0, NB - NI), (1, 0)):
            pieces = []
            for half in range(2):
                pieces.extend(join4(*[state[first + GROUP * half + j].astype(f32) for j in range(GROUP)]))
            isend[side] = jnp.concatenate(pieces, axis=0).astype(bf16)

        @pl.when(sec < sections - 1)
        def _():
            interface_copy(0).start()

        @pl.when(sec > 0)
        def _():
            interface_copy(1).start()

    def await_interfaces():
        @pl.when(sec > 0)
        def _():
            interface_copy(0).wait_recv()

        @pl.when(sec < sections - 1)
        def _():
            interface_copy(1).wait_recv()

    def sweeps():
        def pair(i, carry):
            sweep(st1, st0, bf16)
            sweep(st0, st1, bf16)
            return carry

        lax.fori_loop(0, (ITERS - 2) // 2, pair, 0)

    send_faces(0)
    relayout_matrices()
    first_image(st0)
    face_products(0)
    first_update(0, st1)
    sweeps()
    sweep(st1, st0, bf16)

    send_interfaces(st0)
    for n in range(NB):
        signed[n] = st0[n].astype(f32) * sign[n : n + 1, :]
    send_faces(1)
    first_image(st0)
    face_products(1)
    await_interfaces()
    first_update(1, st1)
    sweeps()
    sweep(st1, signed, f32)

    for i in range(GROUPS):
        for t, piece in enumerate(join4(*[signed[GROUP * i + r] for r in range(GROUP)])):
            out[:, pl.ds(384 * i + LANES * t, LANES)] = piece

    for tick in range(TICKS):

        def sent(d, carry):
            face_copy(tick, d).wait_send()
            return carry

        lax.fori_loop(1, peers, sent, 0)

    @pl.when(sec < sections - 1)
    def _():
        interface_copy(0).wait_send()

    @pl.when(sec > 0)
    def _():
        interface_copy(1).wait_send()


def shards(
    rhs, curl_blocks, block_cols, hole_mask, edge_flip, send_list, send_count, recv_list, dtn_blocks
):
    peers = send_list.shape[2]
    sections = lax.axis_size("sec")
    curl = curl_blocks.reshape(NB, K, ROWS, LANES).transpose(0, 2, 1, 3).reshape(NB, K * ROWS, LANES)
    dtn = dtn_blocks[0, 0].reshape(peers, F, ROWS, LANES).transpose(0, 2, 1, 3).reshape(peers, F * ROWS, LANES)
    smem = pl.BlockSpec(memory_space=pltpu.SMEM)
    vmem = pl.BlockSpec(memory_space=pltpu.VMEM)
    hbm = pl.BlockSpec(memory_space=pl.ANY)
    dma = pltpu.SemaphoreType.DMA
    out = pl.pallas_call(
        lambda *refs: kernel(peers, sections, *refs),
        out_shape=jax.ShapeDtypeStruct((COLS, NB * BS), f32),
        in_specs=[vmem, vmem, smem, smem, smem, smem, smem, hbm, hbm],
        out_specs=vmem,
        scratch_shapes=[
            pltpu.VMEM((NB, K * ROWS, LANES), bf16),
            pltpu.VMEM((peers, F * ROWS, LANES), bf16),
            pltpu.VMEM((4, K * ROWS, LANES), f32),
            pltpu.VMEM((16, BS, LANES), f32),
            pltpu.VMEM((NB, 3 * LANES, LANES), bf16),
            pltpu.VMEM((peers, F, BS, LANES), bf16),
            pltpu.VMEM((NB, COLS, LANES), f32),
            pltpu.VMEM((NB, COLS, LANES), f32),
            pltpu.VMEM((NB, COLS, LANES), f32),
            pltpu.VMEM((NB, COLS, LANES), bf16),
            pltpu.VMEM((NB, COLS, LANES), bf16),
            pltpu.VMEM((NB, COLS, LANES), f32),
            pltpu.VMEM((NB, LANES), f32),
            pltpu.VMEM((3 * GROUPS, LANES), f32),
            pltpu.VMEM((COLS * LANES, LANES), f32),
            pltpu.VMEM((COLS * NB, LANES), f32),
            pltpu.VMEM((NB, LANES), bf16),
            pltpu.VMEM((TICKS, peers, PACK, LANES), bf16),
            pltpu.VMEM((TICKS, peers, PACK, LANES), bf16),
            pltpu.VMEM((2, PACK, LANES), bf16),
            pltpu.VMEM((2, PACK, LANES), bf16),
            dma((CHUNKS,)),
            dma((peers,)),
            dma((TICKS, peers)),
            dma((TICKS, peers)),
            dma((2,)),
            dma((2,)),
        ],
        compiler_params=pltpu.CompilerParams(
            collective_id=0, has_side_effects=True, vmem_limit_bytes=56 << 20
        ),
        name="relay",
    )(
        rhs,
        edge_flip.reshape(3 * GROUPS, LANES),
        block_cols.T,
        hole_mask,
        send_list[0, 0].T,
        send_count[0],
        recv_list[0, 0].T,
        curl,
        dtn,
    )
    return out


def solution(mesh):
    in_specs = (
        P(None, ("sec", "patch")),
        P(("sec", "patch"), None, None),
        P(("sec", "patch"), None),
        P(("sec", "patch")),
        P(("sec", "patch")),
        P("sec", "patch", None, None),
        P("sec", "patch", None),
        P("sec", "patch", None, None),
        P("sec", "patch", None, None, None),
    )
    out_specs = P(None, ("sec", "patch"))
    return jax.shard_map(shards, mesh=mesh, in_specs=in_specs, out_specs=out_specs, check_vma=False)
```

```python
import jax
import jax.numpy as jnp
from jax import lax
from jax.experimental import pallas as pl
from jax.experimental.pallas import tpu as pltpu
from jax.sharding import PartitionSpec as P

BS = 96
COLS = 24
NB = 64
K = 4
F = 8
NI = 8
ITERS = 8
TICKS = 2
LANES = 128
ROWS = BS * BS // LANES
GROUP = 4
GROUPS = NB // GROUP
PACK = 2 * 3 * COLS
COUPLING = 0.85
OCTETS = NB // 8
SIDE = 4
BATCH = 5
ARRIVALS = ((16,), (8, 8))
STEPS = (
    (0, 0), (2, 2), (1, 2), (2, 1), (3, 2), (2, 3), (0, 2), (2, 0),
    (1, 1), (3, 3), (1, 3), (3, 1), (0, 1), (1, 0), (0, 3), (3, 0),
)

f32 = jnp.float32
bf16 = jnp.bfloat16
NN = (((1,), (0,)), ((), ()))


def lanes_of(shape):
    return lax.broadcasted_iota(jnp.int32, shape, len(shape) - 1)


def split4(a, b, c):
    lane = lanes_of(a.shape)
    return (
        a,
        pltpu.roll(jnp.where(lane >= 96, a, b), 32, 1),
        pltpu.roll(jnp.where(lane >= 64, b, c), 64, 1),
        pltpu.roll(c, 96, 1),
    )


def join4(w, x, y, z):
    lane = lanes_of(w.shape)
    x = pltpu.roll(x, 96, 1)
    y = pltpu.roll(y, 64, 1)
    z = pltpu.roll(z, 32, 1)
    return jnp.where(lane < 96, w, x), jnp.where(lane < 64, x, y), jnp.where(lane < 32, y, z)


def kernel(
    peers, sections,
    rhs_in, flip_in, cols, hole, slist, scount, rlist, curl, dtn, out,
    rhs, flip,
    abuf, dbuf, wide, square, dsquare, mats, dmats, src, frc, img, st0, st1, signed, sign, signrow,
    prod, face, onehot, sendbuf, recvbuf, isend, irecv,
    bsem, csem, dsem, ssem, rsem, issem, irsem,
):
    me = lax.axis_index("patch")
    cat = jnp.concatenate
    zeros = jnp.zeros((COLS, LANES), bf16)
    dot = lambda x, y: lax.dot_general(x, y, NN, preferred_element_type=f32)

    def peer(d, sign):
        dx, dy = STEPS[d]
        x = lax.rem(me // SIDE + (dx if sign > 0 else SIDE - dx), SIDE)
        y = lax.rem(lax.rem(me, SIDE) + (dy if sign > 0 else SIDE - dy), SIDE)
        return x * SIDE + y

    sec = lax.axis_index("sec")

    curl_copies = lambda i: pltpu.make_async_copy(
        curl.at[pl.ds(i * 8, 8)],
        abuf.at[pl.ds(i * 8, 8)],
        csem.at[i],
    )
    dtn_copies = lambda i: pltpu.make_async_copy(dtn.at[i], dbuf.at[i], dsem.at[i])

    rhs_copy = pltpu.make_async_copy(rhs_in, rhs, bsem.at[0])
    flip_copy = pltpu.make_async_copy(flip_in, flip, bsem.at[1])
    rhs_copy.start()
    flip_copy.start()
    irecv[...] = jnp.zeros_like(irecv)
    barrier = pltpu.get_barrier_semaphore()
    for d in range(1, peers):
        pl.semaphore_signal(
            barrier, inc=1, device_id={"patch": lax.rem(me + d, peers)}, device_id_type=pl.DeviceIdType.MESH
        )

    for d in (1, sections - 1):
        pl.semaphore_signal(
            barrier, inc=1, device_id={"sec": lax.rem(sec + d, sections)}, device_id_type=pl.DeviceIdType.MESH
        )

    for i in range(OCTETS):
        curl_copies(i).start()
    for i in range(peers):
        dtn_copies(i).start()

    flip_copy.wait()
    signrow[...] = (1 - 2 * flip[...]).astype(f32)
    parts = [signrow[pl.ds(t, GROUPS, stride=3), :] for t in range(3)]
    for r, row in enumerate(split4(*parts)):
        sign[pl.ds(r, GROUPS, stride=4), :] = row

    rhs_copy.wait()
    for i in range(GROUPS):
        parts = [rhs[:, pl.ds(384 * i + LANES * t, LANES)].astype(f32) for t in range(3)]
        for r, row in enumerate(split4(*parts)):
            n = GROUP * i + r
            kept = row * hole[n].astype(f32)
            src[n] = row
            st0[n] = kept.astype(bf16)
            signed[n] = kept * sign[n : n + 1, :]

    pl.semaphore_wait(barrier, peers + 1)

    def face_copy(tick, d):
        return pltpu.make_async_remote_copy(
            src_ref=sendbuf.at[tick, d],
            dst_ref=recvbuf.at[tick, d],
            send_sem=ssem.at[tick, d],
            recv_sem=rsem.at[tick, d],
            device_id={"patch": peer(d, 1)},
            device_id_type=pl.DeviceIdType.MESH,
        )

    def packed(q):
        pieces = []
        for half in range(2):
            blocks = []
            for j in range(GROUP):
                f = GROUP * half + j
                used = jnp.where(f < scount[0, q], 1.0, 0.0).astype(f32)
                blocks.append(signed[slist[f, q]] * used)
            pieces.extend(join4(*blocks))
        return jnp.concatenate(pieces, axis=0).astype(bf16)

    def send_faces(tick):
        for first in range(1, peers, BATCH):
            for d in range(first, first + BATCH):
                sendbuf[tick, d] = packed(peer(d, 1))
            for d in range(first, first + BATCH):
                face_copy(tick, d).start()
        recvbuf[tick, 0] = packed(me)

    def gather(state, n):
        lane = lanes_of((COLS, LANES))
        last = state[cols[3, n]]
        return [jnp.where(lane < BS, state[cols[k, n]], pltpu.roll(last, 96 - 32 * k, 1)) for k in range(3)]

    def images(state, o):
        lane = lanes_of((COLS, LANES))
        xs = [gather(state, 8 * o + i) for i in range(8)]
        front = [cat(x[:2], axis=1) for x in xs]
        low = [cat([x[2], zeros], axis=1) for x in xs[:4]]
        high = [cat([zeros, x[2]], axis=1) for x in xs[4:]]
        first = [
            [dot(cat([front[4 * g + j], front[4 * g + 3]], axis=0), mats[o, 3 * g + j]) for j in range(3)]
            for g in range(2)
        ]
        rest = [dot(cat([low[j], low[3], high[j], high[3]], axis=0), mats[o, 6 + j]) for j in range(3)]
        out = []
        for g in range(2):
            thirds = []
            for j in range(3):
                out.append(first[g][j][:COLS] + rest[j][2 * g * COLS : (2 * g + 1) * COLS])
                third = first[g][j][COLS:] + rest[j][(2 * g + 1) * COLS : (2 * g + 2) * COLS]
                thirds.append(pltpu.roll(third, 32 * j + 32, 1))
            out.append(jnp.where(lane < 32, thirds[0], jnp.where(lane < 64, thirds[1], thirds[2])))
        return out

    def first_image(state):
        values = [images(state, o) for o in range(OCTETS)]
        for o in range(OCTETS):
            for i in range(8):
                img[8 * o + i] = values[o][i]

    def sweep(before, store):
        stores = []
        for o in range(OCTETS):
            for i, value in enumerate(images(before, o)):
                n = 8 * o + i
                stores.append((n, frc[n] - (COUPLING * hole[n].astype(f32)) * value))
        for n, value in stores:
            store(n, value)

    def store_in(ref):
        def store(n, value):
            ref[n] = value.astype(ref.dtype)

        return store

    def store_signed(n, value):
        rounded = value.astype(bf16)
        st0[n] = rounded
        signed[n] = rounded.astype(f32) * sign[n : n + 1, :]

    def relayout_matrices():
        def rows_of(slot, base, stride, count):
            parts = [wide[slot, pl.ds(base + stride * t, count, stride=3 * stride), :] for t in range(3)]
            return split4(*parts)

        def chunk(o, carry):
            lane = lanes_of((COLS // 2, LANES))
            curl_copies(o).wait()
            for u in range(2):
                dtn_copies(2 * o + u).wait()
            for i in range(8):
                wide[i] = abuf[8 * o + i].astype(f32)
            for u in range(2):
                for v in range(2):
                    wide[8 + 2 * u + v] = dbuf[2 * o + u, pl.ds(288 * v, 288)].astype(f32)
            for g in range(2):
                for k in range(K):
                    at = [(g * K + k) * 3 + j for j in range(3)]
                    for j in range(3):
                        for r, row in enumerate(rows_of(4 * g + j, k, K, COLS)):
                            square[at[j], pl.ds(r, COLS, stride=4), :] = row
                    for r, row in enumerate(rows_of(4 * g + 3, k, K, COLS)):
                        for j in range(3):
                            square[at[j], pl.ds(BS + r, 8, stride=4), :] = row[8 * j : 8 * j + 8]
            for u in range(2):
                for f in range(F):
                    for v in range(2):
                        for r, row in enumerate(rows_of(8 + 2 * u + v, f, F, COLS // 2)):
                            row = jnp.where(lane < BS, row, 0.0)
                            dsquare[u * F + f, pl.ds(48 * v + r, COLS // 2, stride=4), :] = row
            for g in range(2):
                for j in range(3):
                    turned = [square[(g * K + k) * 3 + j].T[:BS].astype(bf16) for k in range(K)]
                    mats[o, 3 * g + j] = cat([turned[0], turned[3][:32], turned[1], turned[3][32:64]], axis=0)
                    mats[o, 6 + j, pl.ds(LANES * g, LANES)] = cat([turned[2], turned[3][64:]], axis=0)
            for u in range(2):
                for f in range(F):
                    dmats[2 * o + u, f // 2, pl.ds(LANES * (f % 2), LANES), :BS] = dsquare[u * F + f].T.astype(bf16)
            return carry

        lax.fori_loop(0, OCTETS, chunk, 0)

        lane = lanes_of((1, LANES))
        target = jnp.zeros((1, LANES), jnp.int32)
        for q in range(peers):
            for f in range(F):
                target = jnp.where(lane == q * F + f, rlist[f, q], target)
        rows = lax.broadcasted_iota(jnp.int32, (NB, LANES), 0)
        onehot[...] = jnp.where(rows == target, 1.0, 0.0).astype(bf16)

    def face_product(tick, d):
        q = peer(d, -1)
        got = recvbuf[tick, d].astype(f32)
        for half in range(2):
            base = 72 * half
            rows = split4(got[base : base + 24], got[base + 24 : base + 48], got[base + 48 : base + 72])
            rows = [row.astype(bf16) for row in rows]
            for j in (0, 2):
                f = GROUP * half + j
                both = cat([cat([rows[j], zeros], axis=1), cat([zeros, rows[j + 1]], axis=1)], axis=0)
                value = dot(both, dmats[q, f // 2]).astype(bf16).astype(f32)
                prod[pl.ds(q * F + f, COLS, stride=LANES), :] = value[:COLS]
                prod[pl.ds(q * F + f + 1, COLS, stride=LANES), :] = value[COLS:]

    def face_products(tick):
        begin = 0
        for count in ARRIVALS[tick]:
            for d in range(max(begin, 1), begin + count):
                face_copy(tick, d).wait_recv()
            for d in range(begin, begin + count):
                face_product(tick, d)
            begin += count

        for c in range(COLS):
            face[pl.ds(c * NB, NB), :] = dot(onehot[...], prod[pl.ds(c * LANES, LANES), :].astype(bf16))

    def first_update(tick, after):
        def block(n, extra):
            kept = hole[n].astype(f32)
            forcing = src[n] + face[pl.ds(n, COLS, stride=NB), :]
            if extra is not None:
                forcing = forcing + extra
            forcing = kept * forcing
            frc[n] = forcing
            after[n] = (forcing - (COUPLING * kept) * img[n]).astype(bf16)

        if tick == 0:
            for n in range(NB):
                block(n, None)
        else:
            for side, first in ((0, 0), (1, NB - NI)):
                got = irecv[side].astype(f32)
                for half in range(2):
                    base = 72 * half
                    rows = split4(got[base : base + 24], got[base + 24 : base + 48], got[base + 48 : base + 72])
                    for j in range(GROUP):
                        block(first + GROUP * half + j, rows[j])
            for n in range(NI, NB - NI):
                block(n, None)

    def interface_copy(side):
        return pltpu.make_async_remote_copy(
            src_ref=isend.at[side],
            dst_ref=irecv.at[side],
            send_sem=issem.at[side],
            recv_sem=irsem.at[side],
            device_id={"sec": sec + 1 if side == 0 else sec - 1},
            device_id_type=pl.DeviceIdType.MESH,
        )

    def send_interfaces(state):
        for side, first in ((0, NB - NI), (1, 0)):
            pieces = []
            for half in range(2):
                pieces.extend(join4(*[state[first + GROUP * half + j].astype(f32) for j in range(GROUP)]))
            isend[side] = jnp.concatenate(pieces, axis=0).astype(bf16)

        @pl.when(sec < sections - 1)
        def _():
            interface_copy(0).start()

        @pl.when(sec > 0)
        def _():
            interface_copy(1).start()

    def await_interfaces():
        @pl.when(sec > 0)
        def _():
            interface_copy(0).wait_recv()

        @pl.when(sec < sections - 1)
        def _():
            interface_copy(1).wait_recv()

    def sweeps():
        def pair(i, carry):
            sweep(st1, store_in(st0))
            sweep(st0, store_in(st1))
            return carry

        lax.fori_loop(0, (ITERS - 2) // 2, pair, 0)

    send_faces(0)
    relayout_matrices()
    first_image(st0)
    face_products(0)
    first_update(0, st1)
    sweeps()
    sweep(st1, store_signed)

    send_interfaces(st0)
    send_faces(1)
    first_image(st0)
    face_products(1)
    await_interfaces()
    first_update(1, st1)
    sweeps()
    sweep(st1, store_in(out))

    for tick in range(TICKS):
        for d in range(1, peers):
            face_copy(tick, d).wait_send()

    @pl.when(sec < sections - 1)
    def _():
        interface_copy(0).wait_send()

    @pl.when(sec > 0)
    def _():
        interface_copy(1).wait_send()


def lay_out(state, out):
    for i in range(GROUPS):
        for t, piece in enumerate(join4(*[state[GROUP * i + r] for r in range(GROUP)])):
            out[:, pl.ds(384 * i + LANES * t, LANES)] = piece


def shards(
    rhs, curl_blocks, block_cols, hole_mask, edge_flip, send_list, send_count, recv_list, dtn_blocks
):
    peers = send_list.shape[2]
    sections = lax.axis_size("sec")
    curl = curl_blocks.reshape(NB, K, ROWS, LANES).transpose(0, 2, 1, 3).reshape(NB, K * ROWS, LANES)
    dtn = dtn_blocks[0, 0].reshape(peers, F, ROWS, LANES).transpose(0, 2, 1, 3).reshape(peers, F * ROWS, LANES)
    smem = pl.BlockSpec(memory_space=pltpu.SMEM)
    vmem = pl.BlockSpec(memory_space=pltpu.VMEM)
    hbm = pl.BlockSpec(memory_space=pltpu.HBM)
    dma = pltpu.SemaphoreType.DMA
    state = pl.pallas_call(
        lambda *refs: kernel(peers, sections, *refs),
        out_shape=jax.ShapeDtypeStruct((NB, COLS, LANES), f32),
        in_specs=[hbm, hbm, smem, smem, smem, smem, smem, hbm, hbm],
        out_specs=vmem,
        scratch_shapes=[
            pltpu.VMEM((COLS, NB * BS), bf16),
            pltpu.VMEM((3 * GROUPS, LANES), jnp.int32),
            pltpu.VMEM((NB, K * ROWS, LANES), bf16),
            pltpu.VMEM((peers, F * ROWS, LANES), bf16),
            pltpu.VMEM((12, K * ROWS, LANES), f32),
            pltpu.VMEM((24, LANES, LANES), f32),
            pltpu.VMEM((16, BS, LANES), f32),
            pltpu.VMEM((OCTETS, 9, 2 * LANES, LANES), bf16),
            pltpu.VMEM((peers, F // 2, 2 * LANES, LANES), bf16),
            pltpu.VMEM((NB, COLS, LANES), f32),
            pltpu.VMEM((NB, COLS, LANES), f32),
            pltpu.VMEM((NB, COLS, LANES), f32),
            pltpu.VMEM((NB, COLS, LANES), bf16),
            pltpu.VMEM((NB, COLS, LANES), bf16),
            pltpu.VMEM((NB, COLS, LANES), f32),
            pltpu.VMEM((NB, LANES), f32),
            pltpu.VMEM((3 * GROUPS, LANES), f32),
            pltpu.VMEM((COLS * LANES, LANES), f32),
            pltpu.VMEM((COLS * NB, LANES), f32),
            pltpu.VMEM((NB, LANES), bf16),
            pltpu.VMEM((TICKS, peers, PACK, LANES), bf16),
            pltpu.VMEM((TICKS, peers, PACK, LANES), bf16),
            pltpu.VMEM((2, PACK, LANES), bf16),
            pltpu.VMEM((2, PACK, LANES), bf16),
            dma((2,)),
            dma((OCTETS,)),
            dma((peers,)),
            dma((TICKS, peers)),
            dma((TICKS, peers)),
            dma((2,)),
            dma((2,)),
        ],
        compiler_params=pltpu.CompilerParams(
            collective_id=0, has_side_effects=True, vmem_limit_bytes=52 << 20
        ),
        name="relay",
    )(
        *[
            pltpu.with_memory_space_constraint(x, pltpu.HBM)
            for x in (
                rhs,
                edge_flip.reshape(3 * GROUPS, LANES),
                block_cols.T,
                hole_mask,
                send_list[0, 0].T,
                send_count[0],
                recv_list[0, 0].T,
                curl,
                dtn,
            )
        ]
    )
    return pl.pallas_call(
        lay_out,
        out_shape=jax.ShapeDtypeStruct((COLS, NB * BS), f32),
        in_specs=[vmem],
        out_specs=vmem,
        compiler_params=pltpu.CompilerParams(vmem_limit_bytes=8 << 20),
        name="lay_out",
    )(state)


def solution(mesh):
    in_specs = (
        P(None, ("sec", "patch")),
        P(("sec", "patch"), None, None),
        P(("sec", "patch"), None),
        P(("sec", "patch")),
        P(("sec", "patch")),
        P("sec", "patch", None, None),
        P("sec", "patch", None),
        P("sec", "patch", None, None),
        P("sec", "patch", None, None, None),
    )
    out_specs = P(None, ("sec", "patch"))
    return jax.shard_map(shards, mesh=mesh, in_specs=in_specs, out_specs=out_specs, check_vma=False)
```

```python
import jax
import jax.numpy as jnp
from jax import lax
from jax.experimental import pallas as pl
from jax.experimental.pallas import tpu as pltpu
from jax.sharding import PartitionSpec as P

BS = 96
COLS = 24
NB = 64
K = 4
F = 8
NI = 8
ITERS = 8
TICKS = 2
LANES = 128
ROWS = BS * BS // LANES
GROUP = 4
GROUPS = NB // GROUP
PACK = 2 * 3 * COLS
COUPLING = 0.85
OCTETS = NB // 8
SIDE = 4
SLOT_ROWS = 136
BLOCK_ROWS = 72
BATCH = 5
ARRIVALS = ((16,), (8, 5, 3))
STEPS = (
    (0, 0), (2, 2), (1, 2), (2, 1), (3, 2), (2, 3), (0, 2), (2, 0),
    (1, 1), (3, 3), (1, 3), (3, 1), (0, 1), (1, 0), (0, 3), (3, 0),
)

f32 = jnp.float32
bf16 = jnp.bfloat16
NN = (((1,), (0,)), ((), ()))


def lanes_of(shape):
    return lax.broadcasted_iota(jnp.int32, shape, len(shape) - 1)


def split4(a, b, c):
    lane = lanes_of(a.shape)
    return (
        a,
        pltpu.roll(jnp.where(lane >= 96, a, b), 32, 1),
        pltpu.roll(jnp.where(lane >= 64, b, c), 64, 1),
        pltpu.roll(c, 96, 1),
    )


def join4(w, x, y, z):
    lane = lanes_of(w.shape)
    x = pltpu.roll(x, 96, 1)
    y = pltpu.roll(y, 64, 1)
    z = pltpu.roll(z, 32, 1)
    return jnp.where(lane < 96, w, x), jnp.where(lane < 64, x, y), jnp.where(lane < 32, y, z)


def kernel(
    peers, sections,
    rhs_in, flip_in, cols, hole, slist, scount, rlist, curl, dtn, out,
    rhs, flip,
    abuf, dbuf, wide, square, dsquare, mats, dmats, src, frc, img, st0, st1, signed, sign, signrow,
    prod, face, onehot, sendbuf, recvbuf, isend, irecv,
    bsem, csem, dsem, ssem, rsem, issem, irsem,
):
    me = lax.axis_index("patch")
    cat = jnp.concatenate
    zeros = jnp.zeros((COLS, LANES), bf16)
    dot = lambda x, y: lax.dot_general(x, y, NN, preferred_element_type=f32)

    def peer(d, sign):
        dx, dy = STEPS[d]
        x = lax.rem(me // SIDE + (dx if sign > 0 else SIDE - dx), SIDE)
        y = lax.rem(lax.rem(me, SIDE) + (dy if sign > 0 else SIDE - dy), SIDE)
        return x * SIDE + y

    sec = lax.axis_index("sec")

    curl_copies = lambda i: pltpu.make_async_copy(
        curl.at[pl.ds(i * 8, 8)],
        abuf.at[pl.ds(i * 8, 8)],
        csem.at[i],
    )
    dtn_copies = lambda i: pltpu.make_async_copy(dtn.at[i], dbuf.at[i], dsem.at[i])

    rhs_copy = pltpu.make_async_copy(rhs_in, rhs, bsem.at[0])
    flip_copy = pltpu.make_async_copy(flip_in, flip, bsem.at[1])
    rhs_copy.start()
    flip_copy.start()
    irecv[...] = jnp.zeros_like(irecv)
    barrier = pltpu.get_barrier_semaphore()
    for d in range(1, peers):
        pl.semaphore_signal(
            barrier, inc=1, device_id={"patch": lax.rem(me + d, peers)}, device_id_type=pl.DeviceIdType.MESH
        )

    for d in (1, sections - 1):
        pl.semaphore_signal(
            barrier, inc=1, device_id={"sec": lax.rem(sec + d, sections)}, device_id_type=pl.DeviceIdType.MESH
        )

    for i in range(OCTETS):
        curl_copies(i).start()
    for i in range(peers):
        dtn_copies(i).start()

    flip_copy.wait()
    signrow[: 3 * GROUPS] = (1 - 2 * flip[...]).astype(f32)
    parts = [signrow[pl.ds(t, GROUPS, stride=3), :] for t in range(3)]
    for r, row in enumerate(split4(*parts)):
        sign[pl.ds(r, GROUPS, stride=4), :] = row

    rhs_copy.wait()
    for i in range(GROUPS):
        parts = [rhs[:, pl.ds(384 * i + LANES * t, LANES)].astype(f32) for t in range(3)]
        for r, row in enumerate(split4(*parts)):
            n = GROUP * i + r
            kept = row * hole[n].astype(f32)
            src[n] = row
            st0[n] = kept.astype(bf16)
            signed[n] = kept * sign[n : n + 1, :]

    pl.semaphore_wait(barrier, peers + 1)

    def face_copy(tick, d):
        return pltpu.make_async_remote_copy(
            src_ref=sendbuf.at[tick, d],
            dst_ref=recvbuf.at[tick, d],
            send_sem=ssem.at[tick, d],
            recv_sem=rsem.at[tick, d],
            device_id={"patch": peer(d, 1)},
            device_id_type=pl.DeviceIdType.MESH,
        )

    def packed(q):
        pieces = []
        for half in range(2):
            blocks = []
            for j in range(GROUP):
                f = GROUP * half + j
                used = jnp.where(f < scount[0, q], 1.0, 0.0).astype(f32)
                blocks.append(signed[slist[f, q]] * used)
            pieces.extend(join4(*blocks))
        return jnp.concatenate(pieces, axis=0).astype(bf16)

    def send_faces(tick):
        for first in range(1, peers, BATCH):
            for d in range(first, first + BATCH):
                sendbuf[tick, d] = packed(peer(d, 1))
            for d in range(first, first + BATCH):
                face_copy(tick, d).start()
        recvbuf[tick, 0] = packed(me)

    def gather(state, n):
        lane = lanes_of((COLS, LANES))
        last = state[cols[3, n]]
        return [jnp.where(lane < BS, state[cols[k, n]], pltpu.roll(last, 96 - 32 * k, 1)) for k in range(3)]

    def images(state, o):
        lane = lanes_of((COLS, LANES))
        xs = [gather(state, 8 * o + i) for i in range(8)]
        front = [cat(x[:2], axis=1) for x in xs]
        low = [cat([x[2], zeros], axis=1) for x in xs[:4]]
        high = [cat([zeros, x[2]], axis=1) for x in xs[4:]]
        first = [
            [dot(cat([front[4 * g + j], front[4 * g + 3]], axis=0), mats[o, 3 * g + j]) for j in range(3)]
            for g in range(2)
        ]
        rest = [dot(cat([low[j], low[3], high[j], high[3]], axis=0), mats[o, 6 + j]) for j in range(3)]
        out = []
        for g in range(2):
            thirds = []
            for j in range(3):
                out.append(first[g][j][:COLS] + rest[j][2 * g * COLS : (2 * g + 1) * COLS])
                third = first[g][j][COLS:] + rest[j][(2 * g + 1) * COLS : (2 * g + 2) * COLS]
                thirds.append(pltpu.roll(third, 32 * j + 32, 1))
            out.append(jnp.where(lane < 32, thirds[0], jnp.where(lane < 64, thirds[1], thirds[2])))
        return out

    def first_image(state):
        values = [images(state, o) for o in range(OCTETS)]
        for o in range(OCTETS):
            for i in range(8):
                img[8 * o + i] = values[o][i]

    def sweep(before, store):
        stores = []
        for o in range(OCTETS):
            for i, value in enumerate(images(before, o)):
                n = 8 * o + i
                stores.append((n, frc[n] - (COUPLING * hole[n].astype(f32)) * value))
        for n, value in stores:
            store(n, value)

    def store_in(ref):
        def store(n, value):
            ref[n] = value.astype(ref.dtype)

        return store

    def store_signed(n, value):
        rounded = value.astype(bf16)
        st0[n] = rounded
        signed[n] = rounded.astype(f32) * sign[n : n + 1, :]

    def relayout_matrices():
        def rows_of(slot, base, stride, count):
            parts = [wide[slot, pl.ds(base + stride * t, count, stride=3 * stride), :] for t in range(3)]
            return split4(*parts)

        def chunk(o, carry):
            lane = lanes_of((COLS // 2, LANES))
            curl_copies(o).wait()
            for u in range(2):
                dtn_copies(2 * o + u).wait()
            for i in range(8):
                wide[i, : K * ROWS] = abuf[8 * o + i].astype(f32)
            for u in range(2):
                for v in range(2):
                    wide[8 + 2 * u + v, : K * ROWS] = dbuf[2 * o + u, pl.ds(288 * v, 288)].astype(f32)
            for g in range(2):
                for k in range(K):
                    at = [(g * K + k) * 3 + j for j in range(3)]
                    for j in range(3):
                        for r, row in enumerate(rows_of(4 * g + j, k, K, COLS)):
                            square[at[j], pl.ds(r, COLS, stride=4), :] = row
                    for r, row in enumerate(rows_of(4 * g + 3, k, K, COLS)):
                        for j in range(3):
                            square[at[j], pl.ds(BS + r, 8, stride=4), :] = row[8 * j : 8 * j + 8]
            for u in range(2):
                for f in range(F):
                    for v in range(2):
                        for r, row in enumerate(rows_of(8 + 2 * u + v, f, F, COLS // 2)):
                            row = jnp.where(lane < BS, row, 0.0)
                            dsquare[u * F + f, pl.ds(48 * v + r, COLS // 2, stride=4), :] = row
            for g in range(2):
                for j in range(3):
                    turned = [square[(g * K + k) * 3 + j, :LANES].T[:BS].astype(bf16) for k in range(K)]
                    mats[o, 3 * g + j] = cat([turned[0], turned[3][:32], turned[1], turned[3][32:64]], axis=0)
                    mats[o, 6 + j, pl.ds(LANES * g, LANES)] = cat([turned[2], turned[3][64:]], axis=0)
            for u in range(2):
                for f in range(F):
                    dmats[2 * o + u, f // 2, pl.ds(LANES * (f % 2), LANES), :BS] = dsquare[u * F + f, :BS].T.astype(bf16)
            return carry

        lax.fori_loop(0, OCTETS, chunk, 0)

        lane = lanes_of((1, LANES))
        target = jnp.zeros((1, LANES), jnp.int32)
        for q in range(peers):
            for f in range(F):
                target = jnp.where(lane == q * F + f, rlist[f, q], target)
        rows = lax.broadcasted_iota(jnp.int32, (NB, LANES), 0)
        onehot[...] = jnp.where(rows == target, 1.0, 0.0).astype(bf16)

    def face_product(tick, d):
        q = peer(d, -1)
        got = recvbuf[tick, d].astype(f32)
        for half in range(2):
            base = 72 * half
            rows = split4(got[base : base + 24], got[base + 24 : base + 48], got[base + 48 : base + 72])
            rows = [row.astype(bf16) for row in rows]
            for j in (0, 2):
                f = GROUP * half + j
                both = cat([cat([rows[j], zeros], axis=1), cat([zeros, rows[j + 1]], axis=1)], axis=0)
                value = dot(both, dmats[q, f // 2]).astype(bf16).astype(f32)
                prod[pl.ds(q * F + f, COLS, stride=SLOT_ROWS), :] = value[:COLS]
                prod[pl.ds(q * F + f + 1, COLS, stride=SLOT_ROWS), :] = value[COLS:]

    def face_products(tick):
        begin = 0
        for count in ARRIVALS[tick]:
            for d in range(max(begin, 1), begin + count):
                face_copy(tick, d).wait_recv()
            for d in range(begin, begin + count):
                face_product(tick, d)
            begin += count

        for c in range(COLS):
            face[pl.ds(c * BLOCK_ROWS, NB), :] = dot(
                onehot[...], prod[pl.ds(c * SLOT_ROWS, LANES), :].astype(bf16)
            )

    def first_update(tick, after):
        def block(n, extra):
            kept = hole[n].astype(f32)
            forcing = src[n] + face[pl.ds(n, COLS, stride=BLOCK_ROWS), :]
            if extra is not None:
                forcing = forcing + extra
            forcing = kept * forcing
            frc[n] = forcing
            after[n] = (forcing - (COUPLING * kept) * img[n]).astype(bf16)

        if tick == 0:
            for n in range(NB):
                block(n, None)
        else:
            for side, first in ((0, 0), (1, NB - NI)):
                got = irecv[side].astype(f32)
                for half in range(2):
                    base = 72 * half
                    rows = split4(got[base : base + 24], got[base + 24 : base + 48], got[base + 48 : base + 72])
                    for j in range(GROUP):
                        block(first + GROUP * half + j, rows[j])
            for n in range(NI, NB - NI):
                block(n, None)

    def interface_copy(side):
        return pltpu.make_async_remote_copy(
            src_ref=isend.at[side],
            dst_ref=irecv.at[side],
            send_sem=issem.at[side],
            recv_sem=irsem.at[side],
            device_id={"sec": sec + 1 if side == 0 else sec - 1},
            device_id_type=pl.DeviceIdType.MESH,
        )

    def send_interfaces(state):
        for side, first in ((0, NB - NI), (1, 0)):
            pieces = []
            for half in range(2):
                pieces.extend(join4(*[state[first + GROUP * half + j].astype(f32) for j in range(GROUP)]))
            isend[side] = jnp.concatenate(pieces, axis=0).astype(bf16)

        @pl.when(sec < sections - 1)
        def _():
            interface_copy(0).start()

        @pl.when(sec > 0)
        def _():
            interface_copy(1).start()

    def await_interfaces():
        @pl.when(sec > 0)
        def _():
            interface_copy(0).wait_recv()

        @pl.when(sec < sections - 1)
        def _():
            interface_copy(1).wait_recv()

    def sweeps():
        def pair(i, carry):
            sweep(st1, store_in(st0))
            sweep(st0, store_in(st1))
            return carry

        lax.fori_loop(0, (ITERS - 2) // 2, pair, 0)

    send_faces(0)
    relayout_matrices()
    first_image(st0)
    face_products(0)
    first_update(0, st1)
    sweeps()
    sweep(st1, store_signed)

    send_interfaces(st0)
    send_faces(1)
    first_image(st0)
    face_products(1)
    await_interfaces()
    first_update(1, st1)
    sweeps()
    sweep(st1, store_in(out))

    for tick in range(TICKS):
        for d in range(1, peers):
            face_copy(tick, d).wait_send()

    @pl.when(sec < sections - 1)
    def _():
        interface_copy(0).wait_send()

    @pl.when(sec > 0)
    def _():
        interface_copy(1).wait_send()


def lay_out(state, out):
    for i in range(GROUPS):
        for t, piece in enumerate(join4(*[state[GROUP * i + r] for r in range(GROUP)])):
            out[:, pl.ds(384 * i + LANES * t, LANES)] = piece


def shards(
    rhs, curl_blocks, block_cols, hole_mask, edge_flip, send_list, send_count, recv_list, dtn_blocks
):
    peers = send_list.shape[2]
    sections = lax.axis_size("sec")
    curl = curl_blocks.reshape(NB, K, ROWS, LANES).transpose(0, 2, 1, 3).reshape(NB, K * ROWS, LANES)
    dtn = dtn_blocks[0, 0].reshape(peers, F, ROWS, LANES).transpose(0, 2, 1, 3).reshape(peers, F * ROWS, LANES)
    smem = pl.BlockSpec(memory_space=pltpu.SMEM)
    vmem = pl.BlockSpec(memory_space=pltpu.VMEM)
    hbm = pl.BlockSpec(memory_space=pltpu.HBM)
    dma = pltpu.SemaphoreType.DMA
    state = pl.pallas_call(
        lambda *refs: kernel(peers, sections, *refs),
        out_shape=jax.ShapeDtypeStruct((NB, COLS, LANES), f32),
        in_specs=[hbm, hbm, smem, smem, smem, smem, smem, hbm, hbm],
        out_specs=vmem,
        scratch_shapes=[
            pltpu.VMEM((COLS, NB * BS), bf16),
            pltpu.VMEM((3 * GROUPS, LANES), jnp.int32),
            pltpu.VMEM((NB, K * ROWS, LANES), bf16),
            pltpu.VMEM((peers, F * ROWS, LANES), bf16),
            pltpu.VMEM((12, 408, LANES), f32),
            pltpu.VMEM((24, LANES + 8, LANES), f32),
            pltpu.VMEM((16, 120, LANES), f32),
            pltpu.VMEM((OCTETS, 9, 2 * LANES, LANES), bf16),
            pltpu.VMEM((peers, F // 2, 2 * LANES, LANES), bf16),
            pltpu.VMEM((NB, COLS, LANES), f32),
            pltpu.VMEM((NB, COLS, LANES), f32),
            pltpu.VMEM((NB, COLS, LANES), f32),
            pltpu.VMEM((NB, COLS, LANES), bf16),
            pltpu.VMEM((NB, COLS, LANES), bf16),
            pltpu.VMEM((NB, COLS, LANES), f32),
            pltpu.VMEM((NB + 8, LANES), f32),
            pltpu.VMEM((3 * GROUPS + 8, LANES), f32),
            pltpu.VMEM(((COLS + 1) * SLOT_ROWS, LANES), f32),
            pltpu.VMEM(((COLS + 1) * BLOCK_ROWS, LANES), f32),
            pltpu.VMEM((NB, LANES), bf16),
            pltpu.VMEM((TICKS, peers, PACK, LANES), bf16),
            pltpu.VMEM((TICKS, peers, PACK, LANES), bf16),
            pltpu.VMEM((2, PACK, LANES), bf16),
            pltpu.VMEM((2, PACK, LANES), bf16),
            dma((2,)),
            dma((OCTETS,)),
            dma((peers,)),
            dma((TICKS, peers)),
            dma((TICKS, peers)),
            dma((2,)),
            dma((2,)),
        ],
        compiler_params=pltpu.CompilerParams(
            collective_id=0, has_side_effects=True, vmem_limit_bytes=52 << 20
        ),
        name="relay",
    )(
        *[
            pltpu.with_memory_space_constraint(x, pltpu.HBM)
            for x in (
                rhs,
                edge_flip.reshape(3 * GROUPS, LANES),
                block_cols.T,
                hole_mask,
                send_list[0, 0].T,
                send_count[0],
                recv_list[0, 0].T,
                curl,
                dtn,
            )
        ]
    )
    return pl.pallas_call(
        lay_out,
        out_shape=jax.ShapeDtypeStruct((COLS, NB * BS), f32),
        in_specs=[vmem],
        out_specs=vmem,
        compiler_params=pltpu.CompilerParams(vmem_limit_bytes=8 << 20),
        name="lay_out",
    )(state)


def solution(mesh):
    in_specs = (
        P(None, ("sec", "patch")),
        P(("sec", "patch"), None, None),
        P(("sec", "patch"), None),
        P(("sec", "patch")),
        P(("sec", "patch")),
        P("sec", "patch", None, None),
        P("sec", "patch", None),
        P("sec", "patch", None, None),
        P("sec", "patch", None, None, None),
    )
    out_specs = P(None, ("sec", "patch"))
    return jax.shard_map(shards, mesh=mesh, in_specs=in_specs, out_specs=out_specs, check_vma=False)
```
